256 devices in a mesh: wide: 32 (over y, z_hi, core), narrow: 8 (over z_lo, x).
Axes of the slice: x: 4, y: 4, z: 8 (z_hi: 4, z_lo: 2; z = z_hi * 2 + z_lo), core: 2. Of those that a mesh axis runs over, the one named last changes fastest.
Arguments:
- rhs: float32 [32, 64, 32, 128], P('wide', 'narrow'), may hold values from -16.5 to 16.5
- kappa: float32 [32, 16, 8, 32], P('wide', 'narrow'), may hold values from 0.3 to 3
- low_ratio: float32 [], replicated, may hold values from 0.08 to 0.2
- high_ratio: float32 [], replicated, may hold values from 1.8 to 2.4
Outputs:
- smoothed: float32 [32, 64, 32, 128], P('wide', 'narrow')
- estimate: float32 [], replicated
The draws below stay inside these ranges and needn't reach their ends.
All inputs are finite; a program needn't handle non-finite values.
Results may differ from the reference program's by a relative error of at most 0.0001.
Values sent between devices are 32-bit elements; how exact they have to be, the bound alone decides.
A program may use at most 64 MiB of HBM per device.

```python
import math
from functools import partial
import jax
import jax.numpy as jnp
import numpy as np
from jax import lax

CX = 2
CY = 8
CZ = 32
DEG = 4
SPLIT_Y = 4
SPLIT_Z = 8
CELLS_X = 16
NODES_X = 64
NODES_Y = 32
NODES_Z = 128
N_WIDE = 32
N_NARROW = 8


def draw_rhs(key, part):
    first = jax.random.fold_in(key, 0)
    shape = (N_WIDE, NODES_X, NODES_Y, NODES_Z)
    wide_pos = jnp.arange(N_WIDE, dtype=jnp.float32)[:, None, None, None]
    slab_pos = (jnp.arange(NODES_X, dtype=jnp.int32) // (4 * CX)).astype(jnp.float32)[None, :, None, None]
    level = (wide_pos * N_NARROW + slab_pos) / (N_WIDE * N_NARROW - 1)
    ramp = jnp.exp(level * math.log(3.0))
    base = jnp.clip(jax.random.normal(first, shape, jnp.float32), -5.0, 5.0)
    return base * ramp


def levels(rng, dims, cuts, low, high):
    def one(dim, blocks):
        draws = jax.random.uniform(jax.random.fold_in(jax.random.fold_in(rng, 6), dim), (blocks,), jnp.float32, low / len(cuts), high / len(cuts))
        return jnp.repeat(jnp.exp(draws), dims[dim] // blocks).reshape((-1,) + (1,) * (len(dims) - dim - 1))

    factor_of = one(*cuts[0])
    for cut in cuts[1:]:
        factor_of = factor_of * one(*cut)
    return factor_of


def setup_inputs(seed: int = 0) -> dict:
    seeds = jax.random.split(jax.random.key(seed), 5)
    rhs = draw_rhs(jax.random.fold_in(seeds[4], 71), 0)
    kappa = jnp.clip(jnp.exp(math.log(3.0) - 2.3025851 * jax.random.uniform(seeds[1], (N_WIDE, CELLS_X, CY, CZ), jnp.float32) ** levels(seeds[1], (N_WIDE, CELLS_X, CY, CZ), ((0, 32), (1, 8)), -0.2, 0.2)), 0.3, 3.0)
    low_ratio = jnp.clip(jax.random.uniform(seeds[2], (), jnp.float32, 0.08, 0.2), 0.08, 0.2)
    high_ratio = jnp.clip(jax.random.uniform(seeds[3], (), jnp.float32, 1.8, 2.4), 1.8, 2.4)
    return {"rhs": rhs, "kappa": kappa, "low_ratio": low_ratio, "high_ratio": high_ratio}


def gauss_rule():
    inner_node = math.sqrt(5.0 - 2.0 * math.sqrt(10.0 / 7.0)) / 3.0
    outer_node = math.sqrt(5.0 + 2.0 * math.sqrt(10.0 / 7.0)) / 3.0
    inner_weight = (322.0 + 13.0 * math.sqrt(70.0)) / 900.0
    outer_weight = (322.0 - 13.0 * math.sqrt(70.0)) / 900.0
    gauss = np.array([-outer_node, -inner_node, 0.0, inner_node, outer_node])
    weights = np.array([outer_weight, inner_weight, 128.0 / 225.0, inner_weight, outer_weight])
    return (gauss, weights)

def basis_tables():
    root = math.sqrt(3.0 / 7.0)
    points = (1.0 + np.array([-1.0, -root, 0.0, root, 1.0])) / 2.0
    gauss, weights = gauss_rule()
    quad = (1.0 + gauss) / 2.0
    values = np.zeros((5, 5))
    slopes = np.zeros((5, 5))
    for q in range(5):
        for a in range(5):
            prod = 1.0
            for m in range(5):
                if m != a:
                    prod = prod * (quad[q] - points[m]) / (points[a] - points[m])
            values[q, a] = prod
            total = 0.0
            for l in range(5):
                if l != a:
                    term = 1.0 / (points[a] - points[l])
                    for m in range(5):
                        if m != a and m != l:
                            term = term * (quad[q] - points[m]) / (points[a] - points[m])
                    total = total + term
            slopes[q, a] = total
    return (values, slopes, weights / 2.0)

def unfold(arr):
    count = (arr.shape[2] - 1) // 4
    return jnp.stack([lax.slice_in_dim(arr, i, i + 4 * count - 3, stride=4, axis=2) for i in range(5)], 0)

def unfold_all(field):
    return unfold(unfold(unfold(field)))

def fold(arr):
    moved = jnp.moveaxis(arr, 3, 1)
    count = moved.shape[1]
    rest = moved.shape[2:]
    main = jnp.moveaxis(moved[:4], 0, 1).reshape((4 * count,) + rest)
    main = jnp.concatenate([main, jnp.zeros((1,) + rest, arr.dtype)], 0)
    main = main.at[4::4].add(moved[4])
    return jnp.moveaxis(main, 0, 2)

def fold_all(arr):
    return fold(fold(fold(arr)))

def element_apply(local, coeff):
    values, slopes, weights = basis_tables()
    bmat = jnp.asarray(values, jnp.float32)
    gmat = jnp.asarray(slopes, jnp.float32)
    wvec = jnp.asarray(weights, jnp.float32)
    ein = partial(jnp.einsum, precision=lax.Precision.HIGHEST)
    cells = coeff.shape[0] * coeff.shape[1] * coeff.shape[2]
    field = local.reshape(5, 5, 5, cells)
    bx = ein('qa,abcn->qbcn', bmat, field)
    gx = ein('qa,abcn->qbcn', gmat, field)
    bxby = ein('rb,qbcn->qrcn', bmat, bx)
    bxgy = ein('rb,qbcn->qrcn', gmat, bx)
    gxby = ein('rb,qbcn->qrcn', bmat, gx)
    grad_x = ein('sc,qrcn->qrsn', bmat, gxby)
    grad_y = ein('sc,qrcn->qrsn', bmat, bxgy)
    grad_z = ein('sc,qrcn->qrsn', gmat, bxby)
    weight = wvec[:, None, None, None] * wvec[None, :, None, None] * wvec[None, None, :, None] * coeff.reshape(1, 1, 1, cells)
    back_x = ein('sc,qrsn->qrcn', bmat, grad_x * weight)
    back_y = ein('sc,qrsn->qrcn', bmat, grad_y * weight)
    back_z = ein('sc,qrsn->qrcn', gmat, grad_z * weight)
    mid_x = ein('rb,qrcn->qbcn', bmat, back_x)
    mid_yz = ein('rb,qrcn->qbcn', gmat, back_y) + ein('rb,qrcn->qbcn', bmat, back_z)
    result = ein('qa,qbcn->abcn', gmat, mid_x) + ein('qa,qbcn->abcn', bmat, mid_yz)
    return result.reshape(local.shape)

def element_diag(coeff):
    values, slopes, weights = basis_tables()
    stiff = np.sum(weights[:, None] * slopes * slopes, 0)
    mass = np.sum(weights[:, None] * values * values, 0)
    table = stiff[:, None, None] * mass[None, :, None] * mass[None, None, :] + mass[:, None, None] * stiff[None, :, None] * mass[None, None, :] + mass[:, None, None] * mass[None, None, :] * 0.0 + mass[:, None, None] * mass[None, :, None] * stiff[None, None, :]
    table = jnp.asarray(table, jnp.float32)
    return table[:, :, :, None, None, None] * coeff[None, None, None]

def to_grid(arr):
    depth, rows, cols = (arr.shape[1], arr.shape[2], arr.shape[3])
    grid = arr.reshape(SPLIT_Y, SPLIT_Z, depth, rows, cols).transpose(2, 0, 3, 1, 4)
    return grid.reshape(depth, SPLIT_Y * rows, SPLIT_Z * cols)

def from_grid(grid):
    depth = grid.shape[0]
    rows = grid.shape[1] // SPLIT_Y
    cols = grid.shape[2] // SPLIT_Z
    arr = grid.reshape(depth, SPLIT_Y, rows, SPLIT_Z, cols).transpose(1, 3, 0, 2, 4)
    return arr.reshape(SPLIT_Y * SPLIT_Z, depth, rows, cols)

def assemble(field, coeff_grid, diagonal_only):
    if not diagonal_only:
        padded = jnp.pad(field, ((0, 1), (0, 1), (0, 1)))
    pieces = []
    tail = None
    for slab in range(N_NARROW):
        coeff = coeff_grid[CX * slab:CX * (slab + 1)]
        if diagonal_only:
            local = element_diag(coeff)
        else:
            nodes = padded[4 * CX * slab:4 * CX * (slab + 1) + 1]
            local = element_apply(unfold_all(nodes), coeff)
        summed = fold_all(local)
        if tail is not None:
            summed = summed.at[0].add(tail)
        pieces.append(summed[:-1])
        tail = summed[-1]
    return jnp.concatenate(pieces, 0)[:, :-1, :-1]

def reference(rhs, kappa, low_ratio, high_ratio):
    right = to_grid(rhs)
    coeff_grid = to_grid(kappa)
    inv_diag = 1.0 / assemble(None, coeff_grid, True)
    solution = jnp.zeros_like(right)
    resid = right
    precond = inv_diag * resid
    direction = precond
    gamma = jnp.sum(resid * precond)
    alphas = []
    beta_first = None
    for step in range(2):
        image = assemble(direction, coeff_grid, False)
        alpha = gamma / jnp.sum(direction * image)
        alphas.append(alpha)
        solution = solution + alpha * direction
        resid = resid - alpha * image
        precond = inv_diag * resid
        if step == 0:
            gamma_new = jnp.sum(resid * precond)
            beta_first = gamma_new / gamma
            direction = precond + beta_first * direction
            gamma = gamma_new
    t_first = 1.0 / alphas[0]
    t_cross = jnp.sqrt(beta_first) / alphas[0]
    t_second = 1.0 / alphas[1] + beta_first / alphas[0]
    half = (t_first - t_second) / 2.0
    estimate = (t_first + t_second) / 2.0 + jnp.sqrt(half * half + t_cross * t_cross)
    lower = low_ratio * estimate
    upper = high_ratio * estimate
    theta = (upper + lower) / 2.0
    delta = (upper - lower) / 2.0
    sigma = theta / delta
    rho = 1.0 / sigma
    update = precond / theta
    for step in range(DEG):
        solution = solution + update
        if step + 1 < DEG:
            resid = resid - assemble(update, coeff_grid, False)
            rho_new = 1.0 / (2.0 * sigma - rho)
            update = rho_new * rho * update + 2.0 * rho_new / delta * (inv_diag * resid)
            rho = rho_new
    return (from_grid(solution), estimate)
```

```python
from functools import partial
import math

import jax
import jax.numpy as jnp
import numpy as np
from jax import lax
from jax.experimental import pallas as pl
from jax.experimental.pallas import tpu as pltpu
from jax.sharding import PartitionSpec as P

DEG = 4
SPLIT_Y = 4
MESH = pl.DeviceIdType.MESH
F32 = jnp.float32

SCALE = 0.9


def gauss_rule():
    inner_node = math.sqrt(5.0 - 2.0 * math.sqrt(10.0 / 7.0)) / 3.0
    outer_node = math.sqrt(5.0 + 2.0 * math.sqrt(10.0 / 7.0)) / 3.0
    inner_weight = (322.0 + 13.0 * math.sqrt(70.0)) / 900.0
    outer_weight = (322.0 - 13.0 * math.sqrt(70.0)) / 900.0
    gauss = np.array([-outer_node, -inner_node, 0.0, inner_node, outer_node])
    weights = np.array([outer_weight, inner_weight, 128.0 / 225.0, inner_weight, outer_weight])
    return (gauss, weights)


def basis_tables():
    root = math.sqrt(3.0 / 7.0)
    points = (1.0 + np.array([-1.0, -root, 0.0, root, 1.0])) / 2.0
    gauss, weights = gauss_rule()
    quad = (1.0 + gauss) / 2.0
    values = np.zeros((5, 5))
    slopes = np.zeros((5, 5))
    for q in range(5):
        for a in range(5):
            prod = 1.0
            for m in range(5):
                if m != a:
                    prod = prod * (quad[q] - points[m]) / (points[a] - points[m])
            values[q, a] = prod
            total = 0.0
            for l in range(5):
                if l != a:
                    term = 1.0 / (points[a] - points[l])
                    for m in range(5):
                        if m != a and m != l:
                            term = term * (quad[q] - points[m]) / (points[a] - points[m])
                    total = total + term
            slopes[q, a] = total
    return (values, slopes, weights / 2.0)


def mul(a, b):
    n, k, m = len(a), len(b), len(b[0])
    return [[math.fsum(a[i][l] * b[l][j] for l in range(k)) for j in range(m)] for i in range(n)]


def modes():
    values, slopes, weights = (t.tolist() for t in basis_tables())
    n = 5
    mass = [[math.fsum(weights[q] * values[q][a] * values[q][b] for q in range(n)) for b in range(n)] for a in range(n)]
    stiff = [[math.fsum(weights[q] * slopes[q][a] * slopes[q][b] for q in range(n)) for b in range(n)] for a in range(n)]
    low = [[0.0] * n for _ in range(n)]
    for i in range(n):
        for j in range(i + 1):
            rest = mass[i][j] - math.fsum(low[i][k] * low[j][k] for k in range(j))
            low[i][j] = math.sqrt(rest) if i == j else rest / low[j][j]
    inv = [[0.0] * n for _ in range(n)]
    for c in range(n):
        for i in range(n):
            rest = (1.0 if i == c else 0.0) - math.fsum(low[i][k] * inv[k][c] for k in range(i))
            inv[i][c] = rest / low[i][i]
    trans = [list(t) for t in zip(*inv)]
    work = mul(mul(inv, stiff), trans)
    vecs = [[1.0 if i == j else 0.0 for j in range(n)] for i in range(n)]
    for _ in range(30):
        for p in range(n):
            for q in range(p + 1, n):
                if abs(work[p][q]) < 1e-300:
                    continue
                tau = (work[q][q] - work[p][p]) / (2.0 * work[p][q])
                t = (1.0 if tau >= 0 else -1.0) / (abs(tau) + math.sqrt(1.0 + tau * tau))
                c = 1.0 / math.sqrt(1.0 + t * t)
                s = t * c
                rot = [[1.0 if i == j else 0.0 for j in range(n)] for i in range(n)]
                rot[p][p] = rot[q][q] = c
                rot[p][q], rot[q][p] = s, -s
                work = mul(mul([list(r) for r in zip(*rot)], work), rot)
                vecs = mul(vecs, rot)
    lam = [work[i][i] for i in range(n)]
    vmat = mul([list(r) for r in zip(*vecs)], [list(r) for r in zip(*low)])
    return (
        np.array(vmat),
        np.array(lam),
        np.array([stiff[i][i] for i in range(n)]),
        np.array([mass[i][i] for i in range(n)]),
    )


VMAT, LAM, SDIAG, MDIAG = modes()

ROWS = 320
TILES = 40


def rows_of(i):
    out = []
    for a in range(5):
        x = 4 * i + a
        out.append((x, a, 0))
        out.append((16 + x, a, 32))
        for y in range(1, 32):
            out.append((32 + 32 * a + y, a, y))
    return out


def layer_rows():
    lmats, ldiag = [], []
    for i in range(2):
        mat = np.zeros((200, 192))
        diag = np.zeros((192, 16))
        for row, a, y in rows_of(i):
            for j in range(8):
                b = y - 4 * j
                if 0 <= b <= 4:
                    for p in range(5):
                        for m in range(5):
                            mat[(p * 5 + m) * 8 + j, row] = VMAT[p, a] * VMAT[m, b]
                    diag[row, j] = SDIAG[a] * MDIAG[b] + MDIAG[a] * SDIAG[b]
                    diag[row, 8 + j] = MDIAG[a] * MDIAG[b]
        lmats.append(mat)
        ldiag.append(diag)
    return lmats, ldiag


def z_tables():
    zf = np.zeros((256, 256))
    kc = np.zeros((32, 768))
    for k in range(32):
        for c in range(5):
            z = 4 * k + c
            cols = [z] if z < 128 else list(range(128, 256))
            for r in range(5):
                zf[cols, r * 32 + k] = VMAT[r, c]
            kc[k, [256 + col for col in cols]] = MDIAG[c]
            kc[k, [512 + col for col in cols]] = SDIAG[c]
        for r in range(5):
            kc[k, r * 32 + k] = 1.0
    lamz = np.zeros((8, 256))
    for r in range(5):
        lamz[:, r * 32:r * 32 + 32] = LAM[r]
    return zf, kc, lamz


def opposite(d):
    return tuple(-v for v in d)


DIRS = [(dx, dy, dz) for dz in (-1, 0, 1) for dx in (-1, 0, 1) for dy in (-1, 0, 1) if (dx, dy, dz) != (0, 0, 0)]
DIRS.sort(key=lambda d: -(2 * abs(d[0]) + abs(d[1]) + 2 * abs(d[2])))


def tiles_in(d):
    dx, dy, dz = d
    if dz != 0:
        return 1
    if dx != 0 and dy != 0:
        return 2
    return 7 if dx != 0 else 3


RECV_AT, SEND_AT = {}, {}
_at = 0
for _d in DIRS:
    RECV_AT[_d] = 8 * _at
    _at += tiles_in(_d)
RECV_ROWS = 8 * _at
_at = 2
for _d in DIRS:
    if _d[2] == 0:
        SEND_AT[_d] = 8 * _at
        _at += tiles_in(_d)
    else:
        SEND_AT[_d] = 0 if _d[2] < 0 else 8
SEND_ROWS = 8 * _at


def dot(a, b):
    return lax.dot_general(
        a, b, (((1,), (0,)), ((), ())), precision=lax.Precision.HIGHEST, preferred_element_type=F32
    )


def lanes(shape):
    return lax.broadcasted_iota(jnp.int32, shape, len(shape) - 1)


def row_weight(row, keep_x, keep_y):
    block = row < 32
    place = row & 15
    used = jnp.where(block, jnp.where(place < 9, 1.0, 0.0), jnp.where((row & 31) == 0, 0.0, 1.0))
    used = jnp.where(row < ROWS, used, 0.0)
    top_x = jnp.where(block, jnp.where(place == 8, keep_x, 1.0), jnp.where(row >= 288, keep_x, 1.0))
    top_y = jnp.where(block, jnp.where(row >= 16, keep_y, 1.0), 1.0)
    return used, used * top_x * top_y


def pack_first_lane(a):
    lane = lanes((8, 128))
    out = jnp.where(lane == 0, a[0:8], 0.0)
    for t in range(1, TILES):
        out = jnp.where(lane == t, pltpu.roll(a[8 * t:8 * t + 8], t, 1), out)
    return out


def pack_splat(b):
    lane = lanes((8, 128))
    out = jnp.where(lane == 0, b[0:8], 0.0)
    for t in range(1, TILES):
        out = jnp.where(lane == t, b[8 * t:8 * t + 8], out)
    return out


def kernel(
    sizes, rhs_ref, kappa_ref, low_ref, high_ref, zf_ref, zb_ref, l0_ref, l1_ref, t0_ref, t1_ref, d0_ref, d1_ref,
    kc_ref, lamz_ref, out_ref, est_ref, kw, dia, inva, invz, qa, qz, ya, yz, sb, rb, coef, asend, arecv,
    ssem, rsem, assem, arsem,
):
    nx, ny, nz = sizes
    wide = lax.axis_index("wide")
    bx = lax.axis_index("narrow")
    by = wide // nz
    bz = wide - by * nz

    def exists(d):
        dx, dy, dz = d
        ok = None
        for v, b, n in ((dx, bx, nx), (dy, by, ny), (dz, bz, nz)):
            if v == 0:
                continue
            test = (b > 0) if v < 0 else (b < n - 1)
            ok = test if ok is None else jnp.logical_and(ok, test)
        return ok

    def device(d):
        dx, dy, dz = d
        return {"wide": wide + dy * nz + dz, "narrow": bx + dx}

    def peers(stage):
        n = (nx, ny, nz)[stage]
        me = (bx, by, bz)[stage]
        out = []
        for hop in range(1, n):
            other = lax.rem(me + hop, n)
            if stage == 0:
                out.append({"wide": wide, "narrow": other})
            elif stage == 1:
                out.append({"wide": other * nz + bz, "narrow": bx})
            else:
                out.append({"wide": by * nz + other, "narrow": bx})
        return n, me, out

    rb[...] = jnp.zeros(rb.shape, F32)

    barrier = pltpu.get_barrier_semaphore()
    for d in DIRS:
        @pl.when(exists(d))
        def _():
            pl.semaphore_signal(barrier, inc=1, device_id=device(d), device_id_type=MESH)
    for stage in range(3):
        for other in peers(stage)[2]:
            pl.semaphore_signal(barrier, inc=1, device_id=other, device_id_type=MESH)

    def count(b, n):
        return 1 + jnp.where(b > 0, 1, 0) + jnp.where(b < n - 1, 1, 0)

    expected = count(bx, nx) * count(by, ny) * count(bz, nz) - 1 + (nx - 1) + (ny - 1) + (nz - 1)

    def copy(slot, d):
        n = 8 * tiles_in(d)
        back = opposite(d)
        return pltpu.make_async_remote_copy(
            src_ref=sb.at[slot, pl.ds(SEND_AT[d], n)],
            dst_ref=rb.at[slot, pl.ds(RECV_AT[back], n)],
            send_sem=ssem.at[slot, DIRS.index(d)],
            recv_sem=rsem.at[slot, DIRS.index(back)],
            device_id=device(d),
            device_id_type=MESH,
        )

    def arrival(slot, d):
        n = 8 * tiles_in(d)
        return pltpu.make_async_remote_copy(
            src_ref=sb.at[slot, pl.ds(SEND_AT[d], n)],
            dst_ref=rb.at[slot, pl.ds(RECV_AT[d], n)],
            send_sem=ssem.at[slot, DIRS.index(d)],
            recv_sem=rsem.at[slot, DIRS.index(d)],
            device_id=device(d),
            device_id_type=MESH,
        )

    def fill(slot, a, zu):
        sb[slot, 0:8] = pack_first_lane(a)
        sb[slot, 8:16] = zu
        for d in DIRS:
            dx, dy, dz = d
            if dz != 0:
                continue
            at = SEND_AT[d]
            side = 0 if dx < 0 else 8
            if dy == 0:
                plane = 32 if dx < 0 else 288
                parts = [a[plane:plane + 32], a[side:side + 8], a[16 + side:24 + side]]
            elif dx == 0:
                block = 0 if dy < 0 else 16
                parts = [a[block:block + 16]]
            else:
                block = (0 if dy < 0 else 16) + side
                parts = [a[block:block + 8]]
            for part in parts + [zu]:
                sb[slot, at:at + part.shape[0]] = part
                at += part.shape[0]

    def start(slot):
        for d in DIRS:
            @pl.when(exists(d))
            def _():
                copy(slot, d).start()

    def finish(slot):
        for d in reversed(DIRS):
            @pl.when(exists(d))
            def _():
                copy(slot, d).wait_send()
                arrival(slot, d).wait_recv()

    def got(slot, d, first, n):
        at = RECV_AT[d] + 8 * first
        return rb[slot, at:at + 8 * n]

    def spread(face):
        lane = lanes((8, 128))
        sub = lax.broadcasted_iota(jnp.int32, (8, 128), 0)

        def move(t, by_lanes, mask):
            return jnp.where(mask, pltpu.roll(t, by_lanes % 128, 1), 0.0)

        first = sub == 0
        total = face(-1, 0)
        total = move(total, -32, (lane >= 4) & (lane < 8)) + move(total, -1, first & ((lane == 0) | (lane == 2)))
        right = face(1, 0)
        total = total + move(right, 32, (lane >= 36) & (lane < 40)) + move(right, 1, first & ((lane == 1) | (lane == 3)))
        total = total + move(face(0, -1), -2, lane < 2)
        total = total + move(face(0, 1), 2, (lane == 2) | (lane == 3))
        total = total + move(face(-1, -1), -3, first & (lane == 0))
        total = total + move(face(-1, 1), 1, first & (lane == 2))
        total = total + move(face(1, -1), -1, first & (lane == 1))
        total = total + move(face(1, 1), 3, first & (lane == 3))
        return total

    def combine(slot, a, zu):
        first = lax.broadcasted_iota(jnp.int32, (8, 128), 0) == 0
        lane = lanes((8, 128))

        def only_first(t):
            return jnp.where(first, t, 0.0)

        tiles = [a[8 * t:8 * t + 8] for t in range(TILES)]
        left, right = got(slot, (-1, 0, 0), 0, 6), got(slot, (1, 0, 0), 0, 6)
        below, above = got(slot, (0, -1, 0), 0, 2), got(slot, (0, 1, 0), 0, 2)
        for t in range(4):
            tiles[4 + t] = tiles[4 + t] + left[8 * t:8 * t + 8]
            tiles[36 + t] = tiles[36 + t] + right[8 * t:8 * t + 8]
        tiles[0] = tiles[0] + left[32:40] + below[0:8] + got(slot, (-1, -1, 0), 0, 1)
        tiles[1] = tiles[1] + below[8:16] + only_first(right[32:40] + got(slot, (1, -1, 0), 0, 1))
        tiles[2] = tiles[2] + left[40:48] + above[0:8] + got(slot, (-1, 1, 0), 0, 1)
        tiles[3] = tiles[3] + above[8:16] + only_first(right[40:48] + got(slot, (1, 1, 0), 0, 1))

        low = got(slot, (0, 0, -1), 0, 1) + spread(lambda dx, dy: got(slot, (dx, dy, -1), 0, 1))
        for t in range(TILES):
            moved = low if t == 0 else pltpu.roll(low, 128 - t, 1)
            tiles[t] = tiles[t] + jnp.where(lane == 0, moved, 0.0)
        zu = zu + got(slot, (0, 0, 1), 0, 1) + spread(
            lambda dx, dy: got(slot, (dx, dy, 1), 0, 1) + got(slot, (dx, dy, 0), tiles_in((dx, dy, 0)) - 1, 1)
        )
        return jnp.concatenate(tiles, 0), zu

    def joined(v0, v1):
        return jnp.concatenate(
            [v0[0:32] + v1[0:32], v0[32:160], v0[160:192] + v1[32:64], v1[64:192]], 0
        )

    tiny = jnp.zeros((8, 128), F32)
    row = lax.broadcasted_iota(jnp.int32, (ROWS, 128), 0)
    keep_x = jnp.where(bx == nx - 1, 0.0, 1.0)
    keep_y = jnp.where(by == ny - 1, 0.0, 1.0)
    keep_z = jnp.where(bz == nz - 1, 0.0, 1.0)

    edge = jnp.concatenate([rhs_ref[x, 0:1, :] for x in range(8)], 0)
    not_first = lax.broadcasted_iota(jnp.int32, (32, 128), 0) != 0
    planes = [jnp.where(not_first, rhs_ref[x], 0.0) for x in range(8)]
    right_a = jnp.concatenate([edge, jnp.zeros((24, 128), F32)] + planes + [jnp.zeros((32, 128), F32)], 0)
    fill(3, right_a, tiny)

    table = dot(kappa_ref[...], kc_ref[...])
    parts = []
    for i, ref in ((0, d0_ref), (1, d1_ref)):
        rows = slice(8 * i, 8 * i + 8)
        parts.append(dot(ref[...], jnp.concatenate([table[rows, 256:512], table[rows, 512:768]], 0)))
    diag = joined(parts[0], parts[1])
    diag_a, diag_z = diag[:, :128], pack_splat(diag[:, 128:])
    fill(2, diag_a, diag_z)

    pl.semaphore_wait(barrier, expected)
    start(2)
    start(3)

    for i in range(2):
        for p in range(5):
            for m in range(5):
                at = (p * 5 + m) * 8
                kw[i, at:at + 8, :] = table[8 * i:8 * i + 8, 0:256] * (lamz_ref[...] + float(LAM[p] + LAM[m]))

    finish(2)
    diag_a, diag_z = combine(2, diag_a, diag_z)
    used, weight = row_weight(row, keep_x, keep_y)
    inv_a = weight / (diag_a + (1.0 - used))
    packed_row = 8 * lanes((8, 128)) + lax.broadcasted_iota(jnp.int32, (8, 128), 0)
    used_z, weight_z = row_weight(packed_row, keep_x, keep_y)
    inv_z = weight_z * keep_z / (diag_z + (1.0 - used_z))
    dia[...] = diag_a
    finish(3)
    right_a, right_z = combine(3, right_a, tiny)
    qa[0] = inv_a * right_a
    qz[0] = inv_z * right_z
    inva[...] = inv_a * SCALE
    invz[...] = inv_z * SCALE

    def ar_copy(stage, hop, to):
        return pltpu.make_async_remote_copy(
            src_ref=asend.at[stage],
            dst_ref=arecv.at[stage, (bx, by, bz)[stage]],
            send_sem=assem.at[stage, hop],
            recv_sem=arsem.at[stage, hop],
            device_id=to,
            device_id_type=MESH,
        )

    def ar_start(stage, tile):
        n, me, others = peers(stage)
        asend[stage] = tile
        arecv[stage, me] = tile
        for hop, to in enumerate(others):
            ar_copy(stage, hop, to).start()

    def ar_finish(stage):
        n, me, others = peers(stage)
        for hop, to in enumerate(others):
            c = ar_copy(stage, hop, to)
            c.wait_send()
            c.wait_recv()
        total = arecv[stage, 0]
        for k in range(1, n):
            total = total + arecv[stage, k]
        return total

    def scalars(moments):
        m0, m1, m2, m3 = (jnp.sum(moments[k:k + 1, :], axis=1, keepdims=True) for k in range(4))
        low_ratio, high_ratio = low_ref[...], high_ref[...]
        c = SCALE
        step0 = m0 / (m0 + m1)
        alpha0 = c * step0
        z = [1.0 - step0, -step0]
        gamma1 = z[0] * z[0] * m0 + 2.0 * z[0] * z[1] * m1 + z[1] * z[1] * m2
        beta = gamma1 / m0
        u0, u1 = z[0] + beta, z[1]
        energy = u0 * u0 * (m0 + m1) + 2.0 * u0 * u1 * (m1 + m2) + u1 * u1 * (m2 + m3)
        step1 = gamma1 / energy
        alpha1 = c * step1
        z = [z[0] - step1 * u0, z[1] - step1 * (u0 + u1), -step1 * u1]
        x = [alpha0 + alpha1 * u0, alpha1 * u1]
        t_first = 1.0 / alpha0
        t_cross = jnp.sqrt(beta) / alpha0
        t_second = 1.0 / alpha1 + beta / alpha0
        half = (t_first - t_second) / 2.0
        estimate = (t_first + t_second) / 2.0 + jnp.sqrt(half * half + t_cross * t_cross)
        lower = low_ratio * estimate
        upper = high_ratio * estimate
        theta = (upper + lower) / 2.0
        delta = (upper - lower) / 2.0
        sigma = theta / delta
        rho = 1.0 / sigma
        d = [v / theta for v in z]
        for step in range(DEG):
            x = [(x[k] if k < len(x) else 0.0) + d[k] for k in range(len(d))]
            if step + 1 < DEG:
                td = [(d[k] if k < len(d) else 0.0) + (d[k - 1] if k > 0 else 0.0) for k in range(len(d) + 1)]
                z = [(z[k] if k < len(z) else 0.0) - td[k] * (1.0 / c) for k in range(len(td))]
                rho_new = 1.0 / (2.0 * sigma - rho)
                f, g = rho_new * rho, 2.0 * rho_new / delta
                d = [(f * d[k] if k < len(d) else 0.0) + g * z[k] for k in range(len(z))]
                rho = rho_new
        return x, estimate

    def apply(a, zu):
        tile = lax.broadcasted_iota(jnp.int32, (TILES, 8, 128), 0)
        upper = jnp.where(lanes((TILES, 8, 128)) == tile, jnp.broadcast_to(zu[None], (TILES, 8, 128)), 0.0)
        w = dot(jnp.concatenate([a, upper.reshape(ROWS, 128)], 1), zf_ref[...])
        parts = []
        for i, (lref, tref) in enumerate(((l0_ref, t0_ref), (l1_ref, t1_ref))):
            u = dot(lref[...], jnp.concatenate([w[0:32], w[32 + 128 * i:192 + 128 * i]], 0))
            parts.append(dot(tref[...], u * kw[i]))
        o = dot(joined(parts[0], parts[1]), zb_ref[...])
        return o[:, :128], pack_splat(o[:, 128:])

    def round_(r, carry):
        slot = lax.rem(r, 2)
        a, zu = apply(qa[r - 1], qz[r - 1])
        ya[...] = a
        yz[...] = zu
        fill(slot, a, zu)
        start(slot)

        @pl.when(r == 3)
        def _():
            ar_start(1, ar_finish(0))

        @pl.when(r == 4)
        def _():
            ar_start(2, ar_finish(1))

        @pl.when(r == 5)
        def _():
            x, estimate = scalars(ar_finish(2))
            for k in range(6):
                coef[k] = jnp.broadcast_to(x[k], (8, 128))
            est_ref[...] = estimate

        finish(slot)
        a, zu = combine(slot, ya[...], yz[...])
        qa[r] = inva[...] * a - qa[r - 1]
        qz[r] = invz[...] * zu - qz[r - 1]

        @pl.when(r == 2)
        def _():
            sums = [jnp.zeros((8, 128), F32) for _ in range(4)]
            for t in [0] + list(range(4, 36)):
                rows = slice(8 * t, 8 * t + 8)
                q0, q1, q2, dd = qa[0, rows], qa[1, rows], qa[2, rows], dia[rows]
                d0, d1 = q0 * dd, q1 * dd
                for k, term in enumerate((q0 * d0, q1 * d0, q1 * d1, q2 * d1)):
                    sums[k] = sums[k] + term
            lines = [jnp.sum(s, axis=0, keepdims=True) for s in sums]
            ar_start(0, jnp.concatenate(lines + [jnp.zeros((4, 128), F32)], 0))

        return carry

    lax.fori_loop(1, 6, round_, 0)

    cs = [coef[k] for k in range(6)]

    def mixed(t):
        rows = slice(8 * t, 8 * t + 8)
        total = cs[0] * qa[0, rows]
        for k in range(1, 6):
            total = total + cs[k] * qa[k, rows]
        return total

    for x in range(8):
        for t in range(4):
            out_ref[x, 8 * t:8 * t + 8, :] = mixed(4 + 4 * x + t)
    edge = mixed(0)
    for x in range(8):
        out_ref[x, 0:1, :] = edge[x:x + 1]


def solution(mesh):
    nx = mesh.shape["narrow"]
    ny = SPLIT_Y
    nz = mesh.shape["wide"] // SPLIT_Y
    lmats, ldiag = layer_rows()
    zf, kc, lamz = z_tables()
    zb = np.array(zf.T)
    consts = [zf, zb, lmats[0], lmats[1], lmats[0].T, lmats[1].T, ldiag[0], ldiag[1], kc, lamz]

    def body(rhs, kappa, low_ratio, high_ratio):
        vmem = pl.BlockSpec(memory_space=pltpu.VMEM)
        out, est = pl.pallas_call(
            partial(kernel, (nx, ny, nz)),
            out_shape=(jax.ShapeDtypeStruct((8, 32, 128), F32), jax.ShapeDtypeStruct((1, 1), F32)),
            in_specs=[vmem] * (4 + len(consts)),
            out_specs=(vmem, vmem),
            scratch_shapes=[
                pltpu.VMEM((2, 200, 256), F32),
                pltpu.VMEM((ROWS, 128), F32),
                pltpu.VMEM((ROWS, 128), F32),
                pltpu.VMEM((8, 128), F32),
                pltpu.VMEM((6, ROWS, 128), F32),
                pltpu.VMEM((6, 8, 128), F32),
                pltpu.VMEM((ROWS, 128), F32),
                pltpu.VMEM((8, 128), F32),
                pltpu.VMEM((4, SEND_ROWS, 128), F32),
                pltpu.VMEM((4, RECV_ROWS, 128), F32),
                pltpu.VMEM((6, 8, 128), F32),
                pltpu.VMEM((3, 8, 128), F32),
                pltpu.VMEM((3, 8, 8, 128), F32),
                pltpu.SemaphoreType.DMA((4, 26)),
                pltpu.SemaphoreType.DMA((4, 26)),
                pltpu.SemaphoreType.DMA((3, 8)),
                pltpu.SemaphoreType.DMA((3, 8)),
            ],
            compiler_params=pltpu.CompilerParams(collective_id=0, has_side_effects=True),
        )(
            rhs[0],
            kappa[0].reshape(16, 32),
            low_ratio.reshape(1, 1),
            high_ratio.reshape(1, 1),
            *[jnp.asarray(c, F32) for c in consts],
        )
        return (out[None], est[0, 0])

    return jax.shard_map(
        body,
        mesh=mesh,
        in_specs=(P("wide", "narrow", None, None), P("wide", "narrow", None, None), P(), P()),
        out_specs=(P("wide", "narrow", None, None), P()),
        check_vma=False,
    )
```

```python
from functools import partial
import math

import jax
import jax.numpy as jnp
import numpy as np
from jax import lax
from jax.experimental import pallas as pl
from jax.experimental.pallas import tpu as pltpu
from jax.sharding import PartitionSpec as P

DEG = 4
SPLIT_Y = 4
MESH = pl.DeviceIdType.MESH
F32 = jnp.float32
BF16 = jnp.bfloat16

SCALE = 0.9


def gauss_rule():
    inner_node = math.sqrt(5.0 - 2.0 * math.sqrt(10.0 / 7.0)) / 3.0
    outer_node = math.sqrt(5.0 + 2.0 * math.sqrt(10.0 / 7.0)) / 3.0
    inner_weight = (322.0 + 13.0 * math.sqrt(70.0)) / 900.0
    outer_weight = (322.0 - 13.0 * math.sqrt(70.0)) / 900.0
    gauss = np.array([-outer_node, -inner_node, 0.0, inner_node, outer_node])
    weights = np.array([outer_weight, inner_weight, 128.0 / 225.0, inner_weight, outer_weight])
    return (gauss, weights)


def basis_tables():
    root = math.sqrt(3.0 / 7.0)
    points = (1.0 + np.array([-1.0, -root, 0.0, root, 1.0])) / 2.0
    gauss, weights = gauss_rule()
    quad = (1.0 + gauss) / 2.0
    values = np.zeros((5, 5))
    slopes = np.zeros((5, 5))
    for q in range(5):
        for a in range(5):
            prod = 1.0
            for m in range(5):
                if m != a:
                    prod = prod * (quad[q] - points[m]) / (points[a] - points[m])
            values[q, a] = prod
            total = 0.0
            for l in range(5):
                if l != a:
                    term = 1.0 / (points[a] - points[l])
                    for m in range(5):
                        if m != a and m != l:
                            term = term * (quad[q] - points[m]) / (points[a] - points[m])
                    total = total + term
            slopes[q, a] = total
    return (values, slopes, weights / 2.0)


def mul(a, b):
    n, k, m = len(a), len(b), len(b[0])
    return [[math.fsum(a[i][l] * b[l][j] for l in range(k)) for j in range(m)] for i in range(n)]


def modes():
    values, slopes, weights = (t.tolist() for t in basis_tables())
    n = 5
    mass = [[math.fsum(weights[q] * values[q][a] * values[q][b] for q in range(n)) for b in range(n)] for a in range(n)]
    stiff = [[math.fsum(weights[q] * slopes[q][a] * slopes[q][b] for q in range(n)) for b in range(n)] for a in range(n)]
    low = [[0.0] * n for _ in range(n)]
    for i in range(n):
        for j in range(i + 1):
            rest = mass[i][j] - math.fsum(low[i][k] * low[j][k] for k in range(j))
            low[i][j] = math.sqrt(rest) if i == j else rest / low[j][j]
    inv = [[0.0] * n for _ in range(n)]
    for c in range(n):
        for i in range(n):
            rest = (1.0 if i == c else 0.0) - math.fsum(low[i][k] * inv[k][c] for k in range(i))
            inv[i][c] = rest / low[i][i]
    trans = [list(t) for t in zip(*inv)]
    work = mul(mul(inv, stiff), trans)
    vecs = [[1.0 if i == j else 0.0 for j in range(n)] for i in range(n)]
    for _ in range(30):
        for p in range(n):
            for q in range(p + 1, n):
                if abs(work[p][q]) < 1e-300:
                    continue
                tau = (work[q][q] - work[p][p]) / (2.0 * work[p][q])
                t = (1.0 if tau >= 0 else -1.0) / (abs(tau) + math.sqrt(1.0 + tau * tau))
                c = 1.0 / math.sqrt(1.0 + t * t)
                s = t * c
                rot = [[1.0 if i == j else 0.0 for j in range(n)] for i in range(n)]
                rot[p][p] = rot[q][q] = c
                rot[p][q], rot[q][p] = s, -s
                work = mul(mul([list(r) for r in zip(*rot)], work), rot)
                vecs = mul(vecs, rot)
    lam = [work[i][i] for i in range(n)]
    vmat = mul([list(r) for r in zip(*vecs)], [list(r) for r in zip(*low)])
    return (
        np.array(vmat),
        np.array(lam),
        np.array([stiff[i][i] for i in range(n)]),
        np.array([mass[i][i] for i in range(n)]),
    )


VMAT, LAM, SDIAG, MDIAG = modes()

ROWS = 320
TILES = 40
MODES = 208


def rows_of(i):
    out = []
    for a in range(5):
        x = 4 * i + a
        out.append((x, a, 0))
        out.append((16 + x, a, 32))
        for y in range(1, 32):
            out.append((32 + 32 * a + y, a, y))
    return out


def layer_rows():
    lmats, ldiag = [], []
    for i in range(2):
        mat = np.zeros((MODES, 192))
        diag = np.zeros((192, 16))
        for row, a, y in rows_of(i):
            for j in range(8):
                b = y - 4 * j
                if 0 <= b <= 4:
                    for p in range(5):
                        for m in range(5):
                            mat[(p * 5 + m) * 8 + j, row] = VMAT[p, a] * VMAT[m, b]
                    diag[row, j] = SDIAG[a] * MDIAG[b] + MDIAG[a] * SDIAG[b]
                    diag[row, 8 + j] = MDIAG[a] * MDIAG[b]
        lmats.append(mat)
        ldiag.append(diag)
    return lmats, ldiag


def halves(mat):
    high = np.asarray(mat, np.float32).astype(jnp.bfloat16)
    low = (np.asarray(mat) - high.astype(np.float64)).astype(np.float32).astype(jnp.bfloat16)
    return high, low


def wide_halves(mat):
    high, low = halves(mat)
    return np.concatenate([high, high, low], 1)


def z_tables():
    zf = np.zeros((129, 256))
    kc = np.zeros((32, 768))
    lamz = np.zeros((8, 256))
    for k in range(32):
        for c in range(5):
            z = 4 * k + c
            cols = [z] if z < 128 else list(range(128, 256))
            kc[k, [256 + col for col in cols]] = MDIAG[c]
            kc[k, [512 + col for col in cols]] = SDIAG[c]
            for group in range(7):
                zf[z, group * 32 + k] = VMAT[min(group, 4), c]
        for group in range(7):
            kc[k, group * 32 + k] = 1.0
            lamz[:, group * 32 + k] = LAM[min(group, 4)]
    high, low = halves(zf)
    up = np.concatenate(
        [np.repeat(high[128:], 80, 0), np.repeat(low[128:], 40, 0), np.zeros((8, 256), jnp.bfloat16)], 0
    )
    forward = np.concatenate([high[:128], high[:128], low[:128], up], 0)
    turned = np.zeros((256, 256))
    turned[:, :128] = zf[:128].T
    turned[:, 128:] = zf[128:].T
    high, low = halves(turned)
    last = np.concatenate([high[128:192], low[128:160], np.zeros((32, 256), jnp.bfloat16)], 0)
    backward = np.concatenate([high[:128], high[:128], low[:128], last], 0)
    return forward, backward, kc, lamz


def opposite(d):
    return tuple(-v for v in d)


DIRS = [(dx, dy, dz) for dz in (-1, 0, 1) for dx in (-1, 0, 1) for dy in (-1, 0, 1) if (dx, dy, dz) != (0, 0, 0)]
DIRS.sort(key=lambda d: -(2 * abs(d[0]) + abs(d[1]) + 2 * abs(d[2])))


def tiles_in(d):
    dx, dy, dz = d
    if dz != 0:
        return 1
    if dx != 0 and dy != 0:
        return 2
    return 7 if dx != 0 else 3


RECV_AT, SEND_AT = {}, {}
_at = 0
for _d in DIRS:
    RECV_AT[_d] = 8 * _at
    _at += tiles_in(_d)
RECV_ROWS = 8 * _at
_at = 2
for _d in DIRS:
    if _d[2] == 0:
        SEND_AT[_d] = 8 * _at
        _at += tiles_in(_d)
    else:
        SEND_AT[_d] = 0 if _d[2] < 0 else 8
SEND_ROWS = 8 * _at


def dot(a, b):
    return lax.dot_general(
        a, b, (((1,), (0,)), ((), ())), precision=lax.Precision.HIGHEST, preferred_element_type=F32
    )


def split(x):
    high = x.astype(BF16)
    return high, (x - high.astype(F32)).astype(BF16)


def dot16(a, b):
    return lax.dot_general(a, b, (((1,), (0,)), ((), ())), preferred_element_type=F32)


def lanes(shape):
    return lax.broadcasted_iota(jnp.int32, shape, len(shape) - 1)


def row_weight(row, keep_x, keep_y):
    block = row < 32
    place = row & 15
    used = jnp.where(block, jnp.where(place < 9, 1.0, 0.0), jnp.where((row & 31) == 0, 0.0, 1.0))
    used = jnp.where(row < ROWS, used, 0.0)
    top_x = jnp.where(block, jnp.where(place == 8, keep_x, 1.0), jnp.where(row >= 288, keep_x, 1.0))
    top_y = jnp.where(block, jnp.where(row >= 16, keep_y, 1.0), 1.0)
    return used, used * top_x * top_y


def pack_first_lane(a):
    lane = lanes((8, 128))
    out = jnp.where(lane == 0, a[0:8], 0.0)
    for t in range(1, TILES):
        out = jnp.where(lane == t, pltpu.roll(a[8 * t:8 * t + 8], t, 1), out)
    return out


def pack_splat(b):
    lane = lanes((8, 128))
    out = jnp.where(lane == 0, b[0:8], 0.0)
    for t in range(1, TILES):
        out = jnp.where(lane == t, b[8 * t:8 * t + 8], out)
    return out


def kernel(
    sizes, rhs_ref, kappa_ref, low_ref, high_ref, d0_ref, d1_ref, kc_ref, lamz_ref,
    zf_hbm, zb_hbm, l0_hbm, l1_hbm, t0_hbm, t1_hbm, out_ref, est_ref,
    zf_ref, zb_ref, l0_ref, l1_ref, t0_ref, t1_ref, csem,
    kw, dia, inva, invz, qa, qz, ya, yz, sb, rb, coef, asend, arecv, ssem, rsem, assem, arsem,
):
    nx, ny, nz = sizes
    wide = lax.axis_index("wide")
    bx = lax.axis_index("narrow")
    by = wide // nz
    bz = wide - by * nz

    def exists(d):
        dx, dy, dz = d
        ok = None
        for v, b, n in ((dx, bx, nx), (dy, by, ny), (dz, bz, nz)):
            if v == 0:
                continue
            test = (b > 0) if v < 0 else (b < n - 1)
            ok = test if ok is None else jnp.logical_and(ok, test)
        return ok

    def device(d):
        dx, dy, dz = d
        return {"wide": wide + dy * nz + dz, "narrow": bx + dx}

    def peers(stage):
        n = (nx, ny, nz)[stage]
        me = (bx, by, bz)[stage]
        out = []
        for hop in range(1, n):
            other = lax.rem(me + hop, n)
            if stage == 0:
                out.append({"wide": wide, "narrow": other})
            elif stage == 1:
                out.append({"wide": other * nz + bz, "narrow": bx})
            else:
                out.append({"wide": by * nz + other, "narrow": bx})
        return n, me, out

    tables = [
        pltpu.make_async_copy(src, dst, csem.at[k])
        for k, (src, dst) in enumerate(
            ((zf_hbm, zf_ref), (l0_hbm, l0_ref), (l1_hbm, l1_ref), (t0_hbm, t0_ref), (t1_hbm, t1_ref), (zb_hbm, zb_ref))
        )
    ]
    for table_copy in tables:
        table_copy.start()

    rb[...] = jnp.zeros(rb.shape, F32)

    barrier = pltpu.get_barrier_semaphore()
    for d in DIRS:
        @pl.when(exists(d))
        def _():
            pl.semaphore_signal(barrier, inc=1, device_id=device(d), device_id_type=MESH)
    for stage in range(3):
        for other in peers(stage)[2]:
            pl.semaphore_signal(barrier, inc=1, device_id=other, device_id_type=MESH)

    def count(b, n):
        return 1 + jnp.where(b > 0, 1, 0) + jnp.where(b < n - 1, 1, 0)

    expected = count(bx, nx) * count(by, ny) * count(bz, nz) - 1 + (nx - 1) + (ny - 1) + (nz - 1)

    def copy(slot, d):
        n = 8 * tiles_in(d)
        back = opposite(d)
        return pltpu.make_async_remote_copy(
            src_ref=sb.at[slot, pl.ds(SEND_AT[d], n)],
            dst_ref=rb.at[slot, pl.ds(RECV_AT[back], n)],
            send_sem=ssem.at[slot, DIRS.index(d)],
            recv_sem=rsem.at[slot, DIRS.index(back)],
            device_id=device(d),
            device_id_type=MESH,
        )

    def arrival(slot, d):
        n = 8 * tiles_in(d)
        return pltpu.make_async_remote_copy(
            src_ref=sb.at[slot, pl.ds(SEND_AT[d], n)],
            dst_ref=rb.at[slot, pl.ds(RECV_AT[d], n)],
            send_sem=ssem.at[slot, DIRS.index(d)],
            recv_sem=rsem.at[slot, DIRS.index(d)],
            device_id=device(d),
            device_id_type=MESH,
        )

    def fill(slot, a, zu):
        sb[slot, 0:8] = pack_first_lane(a)
        sb[slot, 8:16] = zu
        for d in DIRS:
            dx, dy, dz = d
            if dz != 0:
                continue
            at = SEND_AT[d]
            side = 0 if dx < 0 else 8
            if dy == 0:
                plane = 32 if dx < 0 else 288
                parts = [a[plane:plane + 32], a[side:side + 8], a[16 + side:24 + side]]
            elif dx == 0:
                block = 0 if dy < 0 else 16
                parts = [a[block:block + 16]]
            else:
                block = (0 if dy < 0 else 16) + side
                parts = [a[block:block + 8]]
            for part in parts + [zu]:
                sb[slot, at:at + part.shape[0]] = part
                at += part.shape[0]

    def start(slot):
        for d in DIRS:
            @pl.when(exists(d))
            def _():
                copy(slot, d).start()

    def sent(slot):
        for d in reversed(DIRS):
            @pl.when(exists(d))
            def _():
                copy(slot, d).wait_send()

    def finish(slot):
        for d in reversed(DIRS):
            @pl.when(exists(d))
            def _():
                arrival(slot, d).wait_recv()

    def got(slot, d, first, n):
        at = RECV_AT[d] + 8 * first
        return rb[slot, at:at + 8 * n]

    def spread(face):
        lane = lanes((8, 128))
        sub = lax.broadcasted_iota(jnp.int32, (8, 128), 0)

        def move(t, by_lanes, mask):
            return jnp.where(mask, pltpu.roll(t, by_lanes % 128, 1), 0.0)

        first = sub == 0
        total = face(-1, 0)
        total = move(total, -32, (lane >= 4) & (lane < 8)) + move(total, -1, first & ((lane == 0) | (lane == 2)))
        right = face(1, 0)
        total = total + move(right, 32, (lane >= 36) & (lane < 40)) + move(right, 1, first & ((lane == 1) | (lane == 3)))
        total = total + move(face(0, -1), -2, lane < 2)
        total = total + move(face(0, 1), 2, (lane == 2) | (lane == 3))
        total = total + move(face(-1, -1), -3, first & (lane == 0))
        total = total + move(face(-1, 1), 1, first & (lane == 2))
        total = total + move(face(1, -1), -1, first & (lane == 1))
        total = total + move(face(1, 1), 3, first & (lane == 3))
        return total

    def combine(slot, a, zu):
        first = lax.broadcasted_iota(jnp.int32, (8, 128), 0) == 0
        lane = lanes((8, 128))

        def only_first(t):
            return jnp.where(first, t, 0.0)

        tiles = [a[8 * t:8 * t + 8] for t in range(TILES)]
        left, right = got(slot, (-1, 0, 0), 0, 6), got(slot, (1, 0, 0), 0, 6)
        below, above = got(slot, (0, -1, 0), 0, 2), got(slot, (0, 1, 0), 0, 2)
        for t in range(4):
            tiles[4 + t] = tiles[4 + t] + left[8 * t:8 * t + 8]
            tiles[36 + t] = tiles[36 + t] + right[8 * t:8 * t + 8]
        tiles[0] = tiles[0] + left[32:40] + below[0:8] + got(slot, (-1, -1, 0), 0, 1)
        tiles[1] = tiles[1] + below[8:16] + only_first(right[32:40] + got(slot, (1, -1, 0), 0, 1))
        tiles[2] = tiles[2] + left[40:48] + above[0:8] + got(slot, (-1, 1, 0), 0, 1)
        tiles[3] = tiles[3] + above[8:16] + only_first(right[40:48] + got(slot, (1, 1, 0), 0, 1))

        low = got(slot, (0, 0, -1), 0, 1) + spread(lambda dx, dy: got(slot, (dx, dy, -1), 0, 1))
        for t in range(TILES):
            moved = low if t == 0 else pltpu.roll(low, 128 - t, 1)
            tiles[t] = tiles[t] + jnp.where(lane == 0, moved, 0.0)
        zu = zu + got(slot, (0, 0, 1), 0, 1) + spread(
            lambda dx, dy: got(slot, (dx, dy, 1), 0, 1) + got(slot, (dx, dy, 0), tiles_in((dx, dy, 0)) - 1, 1)
        )
        return jnp.concatenate(tiles, 0), zu

    def joined(v0, v1):
        return jnp.concatenate(
            [v0[0:32] + v1[0:32], v0[32:160], v0[160:192] + v1[32:64], v1[64:192]], 0
        )

    tiny = jnp.zeros((8, 128), F32)
    row = lax.broadcasted_iota(jnp.int32, (ROWS, 128), 0)
    keep_x = jnp.where(bx == nx - 1, 0.0, 1.0)
    keep_y = jnp.where(by == ny - 1, 0.0, 1.0)
    keep_z = jnp.where(bz == nz - 1, 0.0, 1.0)

    edge = jnp.concatenate([rhs_ref[x, 0:1, :] for x in range(8)], 0)
    not_first = lax.broadcasted_iota(jnp.int32, (32, 128), 0) != 0
    planes = [jnp.where(not_first, rhs_ref[x], 0.0) for x in range(8)]
    right_a = jnp.concatenate([edge, jnp.zeros((24, 128), F32)] + planes + [jnp.zeros((32, 128), F32)], 0)
    fill(3, right_a, tiny)

    table = dot(kappa_ref[...], kc_ref[...])
    parts = []
    for i, ref in ((0, d0_ref), (1, d1_ref)):
        rows = slice(8 * i, 8 * i + 8)
        parts.append(dot(ref[...], jnp.concatenate([table[rows, 256:512], table[rows, 512:768]], 0)))
    diag = joined(parts[0], parts[1])
    diag_a, diag_z = diag[:, :128], pack_splat(diag[:, 128:])
    fill(2, diag_a, diag_z)

    pl.semaphore_wait(barrier, expected)
    start(2)
    start(3)

    for i in range(2):
        for p in range(5):
            for m in range(5):
                at = (p * 5 + m) * 8
                kw[i, at:at + 8, :] = table[8 * i:8 * i + 8, 0:256] * (lamz_ref[...] + float(LAM[p] + LAM[m]))
        kw[i, 200:MODES, :] = jnp.zeros((MODES - 200, 256), F32)

    finish(2)
    diag_a, diag_z = combine(2, diag_a, diag_z)
    used, weight = row_weight(row, keep_x, keep_y)
    inv_a = weight / (diag_a + (1.0 - used))
    packed_row = 8 * lanes((8, 128)) + lax.broadcasted_iota(jnp.int32, (8, 128), 0)
    used_z, weight_z = row_weight(packed_row, keep_x, keep_y)
    inv_z = weight_z * keep_z / (diag_z + (1.0 - used_z))
    dia[...] = diag_a
    finish(3)
    right_a, right_z = combine(3, right_a, tiny)
    qa[0] = inv_a * right_a
    qz[0] = inv_z * right_z
    inva[...] = inv_a * SCALE
    invz[...] = inv_z * SCALE

    def ar_copy(stage, hop, to):
        return pltpu.make_async_remote_copy(
            src_ref=asend.at[stage],
            dst_ref=arecv.at[stage, (bx, by, bz)[stage]],
            send_sem=assem.at[stage, hop],
            recv_sem=arsem.at[stage, hop],
            device_id=to,
            device_id_type=MESH,
        )

    def ar_start(stage, tile):
        n, me, others = peers(stage)
        asend[stage] = tile
        arecv[stage, me] = tile
        for hop, to in enumerate(others):
            ar_copy(stage, hop, to).start()

    def ar_finish(stage):
        n, me, others = peers(stage)
        for hop, to in enumerate(others):
            c = ar_copy(stage, hop, to)
            c.wait_send()
            c.wait_recv()
        total = arecv[stage, 0]
        for k in range(1, n):
            total = total + arecv[stage, k]
        return total

    def scalars(moments):
        m0, m1, m2, m3 = (jnp.sum(moments[k:k + 1, :], axis=1, keepdims=True) for k in range(4))
        low_ratio, high_ratio = low_ref[...], high_ref[...]
        c = SCALE
        step0 = m0 / (m0 + m1)
        alpha0 = c * step0
        z = [1.0 - step0, -step0]
        gamma1 = z[0] * z[0] * m0 + 2.0 * z[0] * z[1] * m1 + z[1] * z[1] * m2
        beta = gamma1 / m0
        u0, u1 = z[0] + beta, z[1]
        energy = u0 * u0 * (m0 + m1) + 2.0 * u0 * u1 * (m1 + m2) + u1 * u1 * (m2 + m3)
        step1 = gamma1 / energy
        alpha1 = c * step1
        z = [z[0] - step1 * u0, z[1] - step1 * (u0 + u1), -step1 * u1]
        x = [alpha0 + alpha1 * u0, alpha1 * u1]
        t_first = 1.0 / alpha0
        t_cross = jnp.sqrt(beta) / alpha0
        t_second = 1.0 / alpha1 + beta / alpha0
        half = (t_first - t_second) / 2.0
        estimate = (t_first + t_second) / 2.0 + jnp.sqrt(half * half + t_cross * t_cross)
        lower = low_ratio * estimate
        upper = high_ratio * estimate
        theta = (upper + lower) / 2.0
        delta = (upper - lower) / 2.0
        sigma = theta / delta
        rho = 1.0 / sigma
        d = [v / theta for v in z]
        for step in range(DEG):
            x = [(x[k] if k < len(x) else 0.0) + d[k] for k in range(len(d))]
            if step + 1 < DEG:
                td = [(d[k] if k < len(d) else 0.0) + (d[k - 1] if k > 0 else 0.0) for k in range(len(d) + 1)]
                z = [(z[k] if k < len(z) else 0.0) - td[k] * (1.0 / c) for k in range(len(td))]
                rho_new = 1.0 / (2.0 * sigma - rho)
                f, g = rho_new * rho, 2.0 * rho_new / delta
                d = [(f * d[k] if k < len(d) else 0.0) + g * z[k] for k in range(len(z))]
                rho = rho_new
        return x, estimate

    def apply(a, zu):
        tile = lax.broadcasted_iota(jnp.int32, (TILES, 8, 128), 0)
        lane = lanes((TILES, 8, 128))
        z_high = zu.astype(BF16).astype(F32)
        z_all = z_high + pltpu.roll(zu - z_high, TILES, 1) + pltpu.roll(z_high, 2 * TILES, 1)
        own = (lane == tile) | (lane == tile + TILES) | (lane == tile + 2 * TILES)
        upper = jnp.where(own, jnp.broadcast_to(z_all[None], (TILES, 8, 128)), 0.0).reshape(ROWS, 128)
        high, low = split(a)
        w = dot16(jnp.concatenate([high, low, high, upper.astype(BF16)], 1), zf_ref[...])
        high, low = split(w)
        parts = []
        for i, (lref, tref) in enumerate(((l0_ref, t0_ref), (l1_ref, t1_ref))):
            here = slice(32 + 128 * i, 192 + 128 * i)
            both = jnp.concatenate([high[0:32], high[here], low[0:32], low[here], high[0:32], high[here]], 0)
            u_high, u_low = split(dot16(lref[...], both) * kw[i])
            parts.append(dot16(tref[...], jnp.concatenate([u_high, u_low, u_high], 0)))
        p = joined(parts[0], parts[1])
        high, low = split(p[:, :128])
        last = p[:, 128:]
        last_high = last.astype(BF16).astype(F32)
        lane = lanes((ROWS, 128))
        last = jnp.where((lane >= 32) & (lane < 64), last - last_high, last_high).astype(BF16)
        o = dot16(jnp.concatenate([high, low, high, last], 1), zb_ref[...])
        return o[:, :128], pack_splat(o[:, 128:])

    def round_(r, carry):
        slot = lax.rem(r, 2)
        a, zu = apply(qa[r - 1], qz[r - 1])
        ya[...] = a
        yz[...] = zu
        fill(slot, a, zu)
        start(slot)

        @pl.when(r == 1)
        def _():
            sent(2)
            sent(3)

        @pl.when(r > 1)
        def _():
            sent(1 - slot)

        @pl.when(r == 5)
        def _():
            sent(slot)

        @pl.when(r == 3)
        def _():
            ar_start(1, ar_finish(0))

        @pl.when(r == 4)
        def _():
            ar_start(2, ar_finish(1))

        @pl.when(r == 5)
        def _():
            x, estimate = scalars(ar_finish(2))
            for k in range(6):
                coef[k] = jnp.broadcast_to(x[k], (8, 128))
            est_ref[...] = estimate

        finish(slot)
        a, zu = combine(slot, ya[...], yz[...])
        qa[r] = inva[...] * a - qa[r - 1]
        qz[r] = invz[...] * zu - qz[r - 1]

        @pl.when(r == 2)
        def _():
            sums = [jnp.zeros((8, 128), F32) for _ in range(4)]
            for t in [0] + list(range(4, 36)):
                rows = slice(8 * t, 8 * t + 8)
                q0, q1, q2, dd = qa[0, rows], qa[1, rows], qa[2, rows], dia[rows]
                d0, d1 = q0 * dd, q1 * dd
                for k, term in enumerate((q0 * d0, q1 * d0, q1 * d1, q2 * d1)):
                    sums[k] = sums[k] + term
            lines = [jnp.sum(s, axis=0, keepdims=True) for s in sums]
            ar_start(0, jnp.concatenate(lines + [jnp.zeros((4, 128), F32)], 0))

        return carry

    for table_copy in tables:
        table_copy.wait()
    lax.fori_loop(1, 6, round_, 0)

    cs = [coef[k] for k in range(6)]

    def mixed(t):
        rows = slice(8 * t, 8 * t + 8)
        total = cs[0] * qa[0, rows]
        for k in range(1, 6):
            total = total + cs[k] * qa[k, rows]
        return total

    for x in range(8):
        for t in range(4):
            out_ref[x, 8 * t:8 * t + 8, :] = mixed(4 + 4 * x + t)
    edge = mixed(0)
    for x in range(8):
        out_ref[x, 0:1, :] = edge[x:x + 1]


def solution(mesh):
    nx = mesh.shape["narrow"]
    ny = SPLIT_Y
    nz = mesh.shape["wide"] // SPLIT_Y
    lmats, ldiag = layer_rows()
    zf, zb, kc, lamz = z_tables()
    consts = [ldiag[0], ldiag[1], kc, lamz]
    tables = [zf, zb] + [wide_halves(m) for m in lmats] + [wide_halves(m.T) for m in lmats]

    def body(rhs, kappa, low_ratio, high_ratio):
        vmem = pl.BlockSpec(memory_space=pltpu.VMEM)
        out, est = pl.pallas_call(
            partial(kernel, (nx, ny, nz)),
            out_shape=(jax.ShapeDtypeStruct((8, 32, 128), F32), jax.ShapeDtypeStruct((1, 1), F32)),
            in_specs=[vmem] * (4 + len(consts)) + [pl.BlockSpec(memory_space=pl.ANY)] * len(tables),
            out_specs=(vmem, vmem),
            scratch_shapes=[pltpu.VMEM(t.shape, BF16) for t in tables] + [
                pltpu.SemaphoreType.DMA((len(tables),)),
                pltpu.VMEM((2, MODES, 256), F32),
                pltpu.VMEM((ROWS, 128), F32),
                pltpu.VMEM((ROWS, 128), F32),
                pltpu.VMEM((8, 128), F32),
                pltpu.VMEM((6, ROWS, 128), F32),
                pltpu.VMEM((6, 8, 128), F32),
                pltpu.VMEM((ROWS, 128), F32),
                pltpu.VMEM((8, 128), F32),
                pltpu.VMEM((4, SEND_ROWS, 128), F32),
                pltpu.VMEM((4, RECV_ROWS, 128), F32),
                pltpu.VMEM((6, 8, 128), F32),
                pltpu.VMEM((3, 8, 128), F32),
                pltpu.VMEM((3, 8, 8, 128), F32),
                pltpu.SemaphoreType.DMA((4, 26)),
                pltpu.SemaphoreType.DMA((4, 26)),
                pltpu.SemaphoreType.DMA((3, 8)),
                pltpu.SemaphoreType.DMA((3, 8)),
            ],
            compiler_params=pltpu.CompilerParams(collective_id=0, has_side_effects=True),
        )(
            rhs[0],
            kappa[0].reshape(16, 32),
            low_ratio.reshape(1, 1),
            high_ratio.reshape(1, 1),
            *[jnp.asarray(c, F32) for c in consts],
            *[jnp.asarray(t) for t in tables],
        )
        return (out[None], est[0, 0])

    return jax.shard_map(
        body,
        mesh=mesh,
        in_specs=(P("wide", "narrow", None, None), P("wide", "narrow", None, None), P(), P()),
        out_specs=(P("wide", "narrow", None, None), P()),
        check_vma=False,
    )
```

```python
from functools import partial
import math

import jax
import jax.numpy as jnp
import numpy as np
from jax import lax
from jax.experimental import pallas as pl
from jax.experimental.pallas import tpu as pltpu
from jax.sharding import PartitionSpec as P

DEG = 4
SPLIT_Y = 4
MESH = pl.DeviceIdType.MESH
F32 = jnp.float32
BF16 = jnp.bfloat16

SCALE = 0.9


def gauss_rule():
    inner_node = math.sqrt(5.0 - 2.0 * math.sqrt(10.0 / 7.0)) / 3.0
    outer_node = math.sqrt(5.0 + 2.0 * math.sqrt(10.0 / 7.0)) / 3.0
    inner_weight = (322.0 + 13.0 * math.sqrt(70.0)) / 900.0
    outer_weight = (322.0 - 13.0 * math.sqrt(70.0)) / 900.0
    gauss = np.array([-outer_node, -inner_node, 0.0, inner_node, outer_node])
    weights = np.array([outer_weight, inner_weight, 128.0 / 225.0, inner_weight, outer_weight])
    return (gauss, weights)


def basis_tables():
    root = math.sqrt(3.0 / 7.0)
    points = (1.0 + np.array([-1.0, -root, 0.0, root, 1.0])) / 2.0
    gauss, weights = gauss_rule()
    quad = (1.0 + gauss) / 2.0
    values = np.zeros((5, 5))
    slopes = np.zeros((5, 5))
    for q in range(5):
        for a in range(5):
            prod = 1.0
            for m in range(5):
                if m != a:
                    prod = prod * (quad[q] - points[m]) / (points[a] - points[m])
            values[q, a] = prod
            total = 0.0
            for l in range(5):
                if l != a:
                    term = 1.0 / (points[a] - points[l])
                    for m in range(5):
                        if m != a and m != l:
                            term = term * (quad[q] - points[m]) / (points[a] - points[m])
                    total = total + term
            slopes[q, a] = total
    return (values, slopes, weights / 2.0)


def mul(a, b):
    n, k, m = len(a), len(b), len(b[0])
    return [[math.fsum(a[i][l] * b[l][j] for l in range(k)) for j in range(m)] for i in range(n)]


def modes():
    values, slopes, weights = (t.tolist() for t in basis_tables())
    n = 5
    mass = [[math.fsum(weights[q] * values[q][a] * values[q][b] for q in range(n)) for b in range(n)] for a in range(n)]
    stiff = [[math.fsum(weights[q] * slopes[q][a] * slopes[q][b] for q in range(n)) for b in range(n)] for a in range(n)]
    low = [[0.0] * n for _ in range(n)]
    for i in range(n):
        for j in range(i + 1):
            rest = mass[i][j] - math.fsum(low[i][k] * low[j][k] for k in range(j))
            low[i][j] = math.sqrt(rest) if i == j else rest / low[j][j]
    inv = [[0.0] * n for _ in range(n)]
    for c in range(n):
        for i in range(n):
            rest = (1.0 if i == c else 0.0) - math.fsum(low[i][k] * inv[k][c] for k in range(i))
            inv[i][c] = rest / low[i][i]
    trans = [list(t) for t in zip(*inv)]
    work = mul(mul(inv, stiff), trans)
    vecs = [[1.0 if i == j else 0.0 for j in range(n)] for i in range(n)]
    for _ in range(30):
        for p in range(n):
            for q in range(p + 1, n):
                if abs(work[p][q]) < 1e-300:
                    continue
                tau = (work[q][q] - work[p][p]) / (2.0 * work[p][q])
                t = (1.0 if tau >= 0 else -1.0) / (abs(tau) + math.sqrt(1.0 + tau * tau))
                c = 1.0 / math.sqrt(1.0 + t * t)
                s = t * c
                rot = [[1.0 if i == j else 0.0 for j in range(n)] for i in range(n)]
                rot[p][p] = rot[q][q] = c
                rot[p][q], rot[q][p] = s, -s
                work = mul(mul([list(r) for r in zip(*rot)], work), rot)
                vecs = mul(vecs, rot)
    lam = [work[i][i] for i in range(n)]
    vmat = mul([list(r) for r in zip(*vecs)], [list(r) for r in zip(*low)])
    return (
        np.array(vmat),
        np.array(lam),
        np.array([stiff[i][i] for i in range(n)]),
        np.array([mass[i][i] for i in range(n)]),
    )


VMAT, LAM, SDIAG, MDIAG = modes()

ROWS = 320
TILES = 40
MODES = 208


def rows_of(i):
    out = []
    for a in range(5):
        x = 4 * i + a
        out.append((x, a, 0))
        out.append((16 + x, a, 32))
        for y in range(1, 32):
            out.append((32 + 32 * a + y, a, y))
    return out


def layer_rows():
    lmats, ldiag = [], []
    for i in range(2):
        mat = np.zeros((MODES, 192))
        diag = np.zeros((192, 16))
        for row, a, y in rows_of(i):
            for j in range(8):
                b = y - 4 * j
                if 0 <= b <= 4:
                    for p in range(5):
                        for m in range(5):
                            mat[(p * 5 + m) * 8 + j, row] = VMAT[p, a] * VMAT[m, b]
                    diag[row, j] = SDIAG[a] * MDIAG[b] + MDIAG[a] * SDIAG[b]
                    diag[row, 8 + j] = MDIAG[a] * MDIAG[b]
        lmats.append(mat)
        ldiag.append(diag)
    return lmats, ldiag


def halves(mat):
    high = np.asarray(mat, np.float32).astype(jnp.bfloat16)
    low = (np.asarray(mat) - high.astype(np.float64)).astype(np.float32).astype(jnp.bfloat16)
    return high, low


def wide_halves(mat):
    high, low = halves(mat)
    return np.concatenate([high, high, low], 1)


def z_tables():
    zf = np.zeros((129, 256))
    kc = np.zeros((32, 768))
    lamz = np.zeros((8, 256))
    for k in range(32):
        for c in range(5):
            z = 4 * k + c
            cols = [z] if z < 128 else list(range(128, 256))
            kc[k, [256 + col for col in cols]] = MDIAG[c]
            kc[k, [512 + col for col in cols]] = SDIAG[c]
            for group in range(7):
                zf[z, group * 32 + k] = VMAT[min(group, 4), c]
        for group in range(7):
            kc[k, group * 32 + k] = 1.0
            lamz[:, group * 32 + k] = LAM[min(group, 4)]
    high, low = halves(zf)
    up = np.concatenate(
        [np.repeat(high[128:], 80, 0), np.repeat(low[128:], 40, 0), np.zeros((8, 256), jnp.bfloat16)], 0
    )
    forward = np.concatenate([high[:128], high[:128], low[:128], up], 0)
    turned = np.zeros((256, 256))
    turned[:, :128] = zf[:128].T
    turned[:, 128:] = zf[128:].T
    high, low = halves(turned)
    last = np.concatenate([high[128:192], low[128:160], np.zeros((32, 256), jnp.bfloat16)], 0)
    backward = np.concatenate([high[:128], high[:128], low[:128], last], 0)
    return forward, backward, kc, lamz


def opposite(d):
    return tuple(-v for v in d)


DIRS = [(dx, dy, dz) for dz in (-1, 0, 1) for dx in (-1, 0, 1) for dy in (-1, 0, 1) if (dx, dy, dz) != (0, 0, 0)]
DIRS.sort(key=lambda d: -(2 * abs(d[0]) + abs(d[1]) + 2 * abs(d[2])))


def tiles_in(d):
    dx, dy, dz = d
    if dz != 0:
        return 1
    if dx != 0 and dy != 0:
        return 2
    return 7 if dx != 0 else 3


RECV_AT, SEND_AT = {}, {}
_at = 0
for _d in DIRS:
    RECV_AT[_d] = 8 * _at
    _at += tiles_in(_d)
RECV_ROWS = 8 * _at
_at = 2
for _d in DIRS:
    if _d[2] == 0:
        SEND_AT[_d] = 8 * _at
        _at += tiles_in(_d)
    else:
        SEND_AT[_d] = 0 if _d[2] < 0 else 8
SEND_ROWS = 8 * _at


def dot(a, b):
    return lax.dot_general(
        a, b, (((1,), (0,)), ((), ())), precision=lax.Precision.HIGHEST, preferred_element_type=F32
    )


def split(x):
    high = x.astype(BF16)
    return high, (x - high.astype(F32)).astype(BF16)


def dot16(a, b):
    return lax.dot_general(a, b, (((1,), (0,)), ((), ())), preferred_element_type=F32)


def lanes(shape):
    return lax.broadcasted_iota(jnp.int32, shape, len(shape) - 1)


def row_weight(row, keep_x, keep_y):
    block = row < 32
    place = row & 15
    used = jnp.where(block, jnp.where(place < 9, 1.0, 0.0), jnp.where((row & 31) == 0, 0.0, 1.0))
    used = jnp.where(row < ROWS, used, 0.0)
    top_x = jnp.where(block, jnp.where(place == 8, keep_x, 1.0), jnp.where(row >= 288, keep_x, 1.0))
    top_y = jnp.where(block, jnp.where(row >= 16, keep_y, 1.0), 1.0)
    return used, used * top_x * top_y


def pack_first_lane(a):
    lane = lanes((8, 128))
    out = jnp.where(lane == 0, a[0:8], 0.0)
    for t in range(1, TILES):
        out = jnp.where(lane == t, pltpu.roll(a[8 * t:8 * t + 8], t, 1), out)
    return out


def pack_splat(b):
    lane = lanes((8, 128))
    out = jnp.where(lane == 0, b[0:8], 0.0)
    for t in range(1, TILES):
        out = jnp.where(lane == t, b[8 * t:8 * t + 8], out)
    return out


def kernel(
    sizes, rhs_ref, kappa_ref, low_ref, high_ref, d0_ref, d1_ref, kc_ref, lamz_ref,
    z_hbm, l_hbm, t_hbm, out_ref, est_ref, z_ref, l_ref, t_ref, csem,
    kw, dia, inva, invz, qa, qz, ya, yz, sb, rb, sb0, rb0, coef, asend, arecv, ssem, rsem, assem, arsem,
):
    nx, ny, nz = sizes
    wide = lax.axis_index("wide")
    bx = lax.axis_index("narrow")
    by = wide // nz
    bz = wide - by * nz

    def exists(d):
        dx, dy, dz = d
        ok = None
        for v, b, n in ((dx, bx, nx), (dy, by, ny), (dz, bz, nz)):
            if v == 0:
                continue
            test = (b > 0) if v < 0 else (b < n - 1)
            ok = test if ok is None else jnp.logical_and(ok, test)
        return ok

    def device(d):
        dx, dy, dz = d
        return {"wide": wide + dy * nz + dz, "narrow": bx + dx}

    def peers(stage):
        n = (nx, ny, nz)[stage]
        me = (bx, by, bz)[stage]
        out = []
        for hop in range(1, n):
            other = lax.rem(me + hop, n)
            if stage == 0:
                out.append({"wide": wide, "narrow": other})
            elif stage == 1:
                out.append({"wide": other * nz + bz, "narrow": bx})
            else:
                out.append({"wide": by * nz + other, "narrow": bx})
        return n, me, out

    tables = [
        pltpu.make_async_copy(src, dst, csem.at[k])
        for k, (src, dst) in enumerate(
            ((z_hbm, z_ref), (l_hbm, l_ref), (t_hbm, t_ref))
        )
    ]
    for table_copy in tables:
        table_copy.start()

    rb[...] = jnp.zeros(rb.shape, F32)
    rb0[...] = jnp.zeros(rb0.shape, F32)

    barrier = pltpu.get_barrier_semaphore()
    for d in DIRS:
        @pl.when(exists(d))
        def _():
            pl.semaphore_signal(barrier, inc=1, device_id=device(d), device_id_type=MESH)
    for stage in range(3):
        for other in peers(stage)[2]:
            pl.semaphore_signal(barrier, inc=1, device_id=other, device_id_type=MESH)

    def count(b, n):
        return 1 + jnp.where(b > 0, 1, 0) + jnp.where(b < n - 1, 1, 0)

    expected = count(bx, nx) * count(by, ny) * count(bz, nz) - 1 + (nx - 1) + (ny - 1) + (nz - 1)

    def transfer(r, d, landing):
        n = 8 * tiles_in(d)
        slot = lax.rem(r, 2) if r is not None else 0
        if r is None:
            src, dst = sb0.at[pl.ds(2 * SEND_AT[d], 2 * n)], rb0.at[pl.ds(2 * RECV_AT[landing], 2 * n)]
        else:
            src, dst = sb.at[slot, pl.ds(SEND_AT[d], n)], rb.at[slot, pl.ds(RECV_AT[landing], n)]
        return pltpu.make_async_remote_copy(
            src_ref=src,
            dst_ref=dst,
            send_sem=ssem.at[DIRS.index(d)],
            recv_sem=rsem.at[slot, DIRS.index(landing)],
            device_id=device(d),
            device_id_type=MESH,
        )

    def wanted(r, d, down):
        if r is None or all(v * down <= 0 for v in d):
            return exists(d)
        return jnp.logical_and(exists(d), r < 5)

    def start(r):
        for d in DIRS:
            @pl.when(wanted(r, d, -1))
            def _():
                transfer(r, d, opposite(d)).start()

    def finish(r):
        for d in reversed(DIRS):
            @pl.when(wanted(r, d, -1))
            def _():
                transfer(r, d, opposite(d)).wait_send()
        for d in reversed(DIRS):
            @pl.when(wanted(r, d, 1))
            def _():
                transfer(r, d, d).wait_recv()

    def messages(a, zu):
        out = {0: [pack_first_lane(a)], 8: [zu]}
        for d in DIRS:
            dx, dy, dz = d
            if dz != 0:
                continue
            side = 0 if dx < 0 else 8
            if dy == 0:
                plane = 32 if dx < 0 else 288
                parts = [a[plane:plane + 32], a[side:side + 8], a[16 + side:24 + side]]
            elif dx == 0:
                block = 0 if dy < 0 else 16
                parts = [a[block:block + 16]]
            else:
                block = (0 if dy < 0 else 16) + side
                parts = [a[block:block + 8]]
            out[SEND_AT[d]] = parts + [zu]
        return out

    def fill(slot, a, zu):
        for at, parts in messages(a, zu).items():
            for part in parts:
                sb[slot, at:at + part.shape[0]] = part
                at += part.shape[0]

    def fill_both(pairs):
        for which, (a, zu) in enumerate(pairs):
            for at, parts in messages(a, zu).items():
                size = sum(part.shape[0] for part in parts)
                at = 2 * at + which * size
                for part in parts:
                    sb0[at:at + part.shape[0]] = part
                    at += part.shape[0]

    def from_slot(slot):
        def got(d, first, n):
            at = RECV_AT[d] + 8 * first
            return rb[slot, at:at + 8 * n]

        return got

    def from_first(which):
        def got(d, first, n):
            at = 2 * RECV_AT[d] + 8 * (which * tiles_in(d) + first)
            return rb0[at:at + 8 * n]

        return got

    def spread(face):
        lane = lanes((8, 128))
        sub = lax.broadcasted_iota(jnp.int32, (8, 128), 0)

        def move(t, by_lanes, mask):
            return jnp.where(mask, pltpu.roll(t, by_lanes % 128, 1), 0.0)

        first = sub == 0
        total = face(-1, 0)
        total = move(total, -32, (lane >= 4) & (lane < 8)) + move(total, -1, first & ((lane == 0) | (lane == 2)))
        right = face(1, 0)
        total = total + move(right, 32, (lane >= 36) & (lane < 40)) + move(right, 1, first & ((lane == 1) | (lane == 3)))
        total = total + move(face(0, -1), -2, lane < 2)
        total = total + move(face(0, 1), 2, (lane == 2) | (lane == 3))
        total = total + move(face(-1, -1), -3, first & (lane == 0))
        total = total + move(face(-1, 1), 1, first & (lane == 2))
        total = total + move(face(1, -1), -1, first & (lane == 1))
        total = total + move(face(1, 1), 3, first & (lane == 3))
        return total

    def combine(got, a, zu):
        first = lax.broadcasted_iota(jnp.int32, (8, 128), 0) == 0
        lane = lanes((8, 128))

        def only_first(t):
            return jnp.where(first, t, 0.0)

        tiles = [a[8 * t:8 * t + 8] for t in range(TILES)]
        left, right = got((-1, 0, 0), 0, 6), got((1, 0, 0), 0, 6)
        below, above = got((0, -1, 0), 0, 2), got((0, 1, 0), 0, 2)
        for t in range(4):
            tiles[4 + t] = tiles[4 + t] + left[8 * t:8 * t + 8]
            tiles[36 + t] = tiles[36 + t] + right[8 * t:8 * t + 8]
        tiles[0] = tiles[0] + left[32:40] + below[0:8] + got((-1, -1, 0), 0, 1)
        tiles[1] = tiles[1] + below[8:16] + only_first(right[32:40] + got((1, -1, 0), 0, 1))
        tiles[2] = tiles[2] + left[40:48] + above[0:8] + got((-1, 1, 0), 0, 1)
        tiles[3] = tiles[3] + above[8:16] + only_first(right[40:48] + got((1, 1, 0), 0, 1))

        low = got((0, 0, -1), 0, 1) + spread(lambda dx, dy: got((dx, dy, -1), 0, 1))
        for t in range(TILES):
            moved = low if t == 0 else pltpu.roll(low, 128 - t, 1)
            tiles[t] = tiles[t] + jnp.where(lane == 0, moved, 0.0)
        zu = zu + got((0, 0, 1), 0, 1) + spread(
            lambda dx, dy: got((dx, dy, 1), 0, 1) + got((dx, dy, 0), tiles_in((dx, dy, 0)) - 1, 1)
        )
        return jnp.concatenate(tiles, 0), zu

    def joined(v0, v1):
        return jnp.concatenate(
            [v0[0:32] + v1[0:32], v0[32:160], v0[160:192] + v1[32:64], v1[64:192]], 0
        )

    tiny = jnp.zeros((8, 128), F32)
    row = lax.broadcasted_iota(jnp.int32, (ROWS, 128), 0)
    keep_x = jnp.where(bx == nx - 1, 0.0, 1.0)
    keep_y = jnp.where(by == ny - 1, 0.0, 1.0)
    keep_z = jnp.where(bz == nz - 1, 0.0, 1.0)

    edge = jnp.concatenate([rhs_ref[x, 0:1, :] for x in range(8)], 0)
    not_first = lax.broadcasted_iota(jnp.int32, (32, 128), 0) != 0
    planes = [jnp.where(not_first, rhs_ref[x], 0.0) for x in range(8)]
    right_a = jnp.concatenate([edge, jnp.zeros((24, 128), F32)] + planes + [jnp.zeros((32, 128), F32)], 0)

    table = dot(kappa_ref[...], kc_ref[...])
    parts = []
    for i, ref in ((0, d0_ref), (1, d1_ref)):
        rows = slice(8 * i, 8 * i + 8)
        parts.append(dot(ref[...], jnp.concatenate([table[rows, 256:512], table[rows, 512:768]], 0)))
    diag = joined(parts[0], parts[1])
    diag_a, diag_z = diag[:, :128], pack_splat(diag[:, 128:])
    fill_both(((diag_a, diag_z), (right_a, tiny)))

    pl.semaphore_wait(barrier, expected)
    start(None)

    for i in range(2):
        for p in range(5):
            for m in range(5):
                at = (p * 5 + m) * 8
                kw[i, at:at + 8, :] = table[8 * i:8 * i + 8, 0:256] * (lamz_ref[...] + float(LAM[p] + LAM[m]))
        kw[i, 200:MODES, :] = jnp.zeros((MODES - 200, 256), F32)

    finish(None)
    diag_a, diag_z = combine(from_first(0), diag_a, diag_z)
    used, weight = row_weight(row, keep_x, keep_y)
    inv_a = weight / (diag_a + (1.0 - used))
    packed_row = 8 * lanes((8, 128)) + lax.broadcasted_iota(jnp.int32, (8, 128), 0)
    used_z, weight_z = row_weight(packed_row, keep_x, keep_y)
    inv_z = weight_z * keep_z / (diag_z + (1.0 - used_z))
    dia[...] = diag_a
    right_a, right_z = combine(from_first(1), right_a, tiny)
    qa[0] = inv_a * right_a
    qz[0] = inv_z * right_z
    inva[...] = inv_a * SCALE
    invz[...] = inv_z * SCALE

    def ar_copy(stage, hop, to):
        return pltpu.make_async_remote_copy(
            src_ref=asend.at[stage],
            dst_ref=arecv.at[stage, (bx, by, bz)[stage]],
            send_sem=assem.at[hop],
            recv_sem=arsem.at[(0, nx, nx + ny)[stage] + hop],
            device_id=to,
            device_id_type=MESH,
        )

    def ar_start(stage, tile):
        n, me, others = peers(stage)
        asend[stage] = tile
        arecv[stage, me] = tile
        for hop, to in enumerate(others):
            ar_copy(stage, hop, to).start()

    def ar_finish(stage):
        n, me, others = peers(stage)
        for hop, to in enumerate(others):
            c = ar_copy(stage, hop, to)
            c.wait_send()
            c.wait_recv()
        total = arecv[stage, 0]
        for k in range(1, n):
            total = total + arecv[stage, k]
        return total

    def scalars(moments):
        m0, m1, m2, m3 = (jnp.sum(moments[k:k + 1, :], axis=1, keepdims=True) for k in range(4))
        low_ratio, high_ratio = low_ref[...], high_ref[...]
        c = SCALE
        step0 = m0 / (m0 + m1)
        alpha0 = c * step0
        z = [1.0 - step0, -step0]
        gamma1 = z[0] * z[0] * m0 + 2.0 * z[0] * z[1] * m1 + z[1] * z[1] * m2
        beta = gamma1 / m0
        u0, u1 = z[0] + beta, z[1]
        energy = u0 * u0 * (m0 + m1) + 2.0 * u0 * u1 * (m1 + m2) + u1 * u1 * (m2 + m3)
        step1 = gamma1 / energy
        alpha1 = c * step1
        z = [z[0] - step1 * u0, z[1] - step1 * (u0 + u1), -step1 * u1]
        x = [alpha0 + alpha1 * u0, alpha1 * u1]
        t_first = 1.0 / alpha0
        t_cross = jnp.sqrt(beta) / alpha0
        t_second = 1.0 / alpha1 + beta / alpha0
        half = (t_first - t_second) / 2.0
        estimate = (t_first + t_second) / 2.0 + jnp.sqrt(half * half + t_cross * t_cross)
        lower = low_ratio * estimate
        upper = high_ratio * estimate
        theta = (upper + lower) / 2.0
        delta = (upper - lower) / 2.0
        sigma = theta / delta
        rho = 1.0 / sigma
        d = [v / theta for v in z]
        for step in range(DEG):
            x = [(x[k] if k < len(x) else 0.0) + d[k] for k in range(len(d))]
            if step + 1 < DEG:
                td = [(d[k] if k < len(d) else 0.0) + (d[k - 1] if k > 0 else 0.0) for k in range(len(d) + 1)]
                z = [(z[k] if k < len(z) else 0.0) - td[k] * (1.0 / c) for k in range(len(td))]
                rho_new = 1.0 / (2.0 * sigma - rho)
                f, g = rho_new * rho, 2.0 * rho_new / delta
                d = [(f * d[k] if k < len(d) else 0.0) + g * z[k] for k in range(len(z))]
                rho = rho_new
        return x, estimate

    def apply(a, zu):
        tile = lax.broadcasted_iota(jnp.int32, (TILES, 8, 128), 0)
        lane = lanes((TILES, 8, 128))
        z_high = zu.astype(BF16).astype(F32)
        z_all = z_high + pltpu.roll(zu - z_high, TILES, 1) + pltpu.roll(z_high, 2 * TILES, 1)
        own = (lane == tile) | (lane == tile + TILES) | (lane == tile + 2 * TILES)
        upper = jnp.where(own, jnp.broadcast_to(z_all[None], (TILES, 8, 128)), 0.0).reshape(ROWS, 128)
        high, low = split(a)
        w = dot16(jnp.concatenate([high, low, high, upper.astype(BF16)], 1), z_ref[0])
        high, low = split(w)
        parts = []
        for i in range(2):
            here = slice(32 + 128 * i, 192 + 128 * i)
            both = jnp.concatenate([high[0:32], high[here], low[0:32], low[here], high[0:32], high[here]], 0)
            u_high, u_low = split(dot16(l_ref[i], both) * kw[i])
            parts.append(dot16(t_ref[i], jnp.concatenate([u_high, u_low, u_high], 0)))
        p = joined(parts[0], parts[1])
        high, low = split(p[:, :128])
        last = p[:, 128:]
        last_high = last.astype(BF16).astype(F32)
        lane = lanes((ROWS, 128))
        last = jnp.where((lane >= 32) & (lane < 64), last - last_high, last_high).astype(BF16)
        o = dot16(jnp.concatenate([high, low, high, last], 1), z_ref[1])
        return o[:, :128], pack_splat(o[:, 128:])

    def round_(r, carry):
        slot = lax.rem(r, 2)
        a, zu = apply(qa[r - 1], qz[r - 1])
        ya[...] = a
        yz[...] = zu
        fill(slot, a, zu)
        start(r)

        @pl.when(r == 3)
        def _():
            ar_start(1, ar_finish(0))

        @pl.when(r == 4)
        def _():
            ar_start(2, ar_finish(1))

        @pl.when(r == 5)
        def _():
            x, estimate = scalars(ar_finish(2))
            for k in range(6):
                coef[k] = jnp.broadcast_to(x[k], (8, 128))
            est_ref[...] = estimate

        finish(r)
        a, zu = combine(from_slot(slot), ya[...], yz[...])
        qa[r] = inva[...] * a - qa[r - 1]
        qz[r] = invz[...] * zu - qz[r - 1]

        @pl.when(r == 2)
        def _():
            sums = [jnp.zeros((8, 128), F32) for _ in range(4)]
            for t in [0] + list(range(4, 36)):
                rows = slice(8 * t, 8 * t + 8)
                q0, q1, q2, dd = qa[0, rows], qa[1, rows], qa[2, rows], dia[rows]
                d0, d1 = q0 * dd, q1 * dd
                for k, term in enumerate((q0 * d0, q1 * d0, q1 * d1, q2 * d1)):
                    sums[k] = sums[k] + term
            lines = [jnp.sum(s, axis=0, keepdims=True) for s in sums]
            ar_start(0, jnp.concatenate(lines + [jnp.zeros((4, 128), F32)], 0))

        return carry

    for table_copy in tables:
        table_copy.wait()
    lax.fori_loop(1, 6, round_, 0)

    cs = [coef[k] for k in range(6)]

    def mixed(t):
        rows = slice(8 * t, 8 * t + 8)
        total = cs[0] * qa[0, rows]
        for k in range(1, 6):
            total = total + cs[k] * qa[k, rows]
        return total

    for x in range(8):
        for t in range(4):
            out_ref[x, 8 * t:8 * t + 8, :] = mixed(4 + 4 * x + t)
    edge = mixed(0)
    for x in range(8):
        out_ref[x, 0:1, :] = edge[x:x + 1]


def solution(mesh):
    nx = mesh.shape["narrow"]
    ny = SPLIT_Y
    nz = mesh.shape["wide"] // SPLIT_Y
    lmats, ldiag = layer_rows()
    zf, zb, kc, lamz = z_tables()
    consts = [ldiag[0], ldiag[1], kc, lamz]
    tables = [np.stack([zf, zb]), np.stack([wide_halves(m) for m in lmats]), np.stack([wide_halves(m.T) for m in lmats])]

    def body(rhs, kappa, low_ratio, high_ratio):
        vmem = pl.BlockSpec(memory_space=pltpu.VMEM)
        out, est = pl.pallas_call(
            partial(kernel, (nx, ny, nz)),
            out_shape=(jax.ShapeDtypeStruct((8, 32, 128), F32), jax.ShapeDtypeStruct((1, 1), F32)),
            in_specs=[vmem] * (4 + len(consts)) + [pl.BlockSpec(memory_space=pl.ANY)] * len(tables),
            out_specs=(vmem, vmem),
            scratch_shapes=[pltpu.VMEM(t.shape, BF16) for t in tables] + [
                pltpu.SemaphoreType.DMA((len(tables),)),
                pltpu.VMEM((2, MODES, 256), F32),
                pltpu.VMEM((ROWS, 128), F32),
                pltpu.VMEM((ROWS, 128), F32),
                pltpu.VMEM((8, 128), F32),
                pltpu.VMEM((6, ROWS, 128), F32),
                pltpu.VMEM((6, 8, 128), F32),
                pltpu.VMEM((ROWS, 128), F32),
                pltpu.VMEM((8, 128), F32),
                pltpu.VMEM((2, SEND_ROWS, 128), F32),
                pltpu.VMEM((2, RECV_ROWS, 128), F32),
                pltpu.VMEM((2 * SEND_ROWS, 128), F32),
                pltpu.VMEM((2 * RECV_ROWS, 128), F32),
                pltpu.VMEM((6, 8, 128), F32),
                pltpu.VMEM((3, 8, 128), F32),
                pltpu.VMEM((3, 8, 8, 128), F32),
                pltpu.SemaphoreType.DMA((26,)),
                pltpu.SemaphoreType.DMA((2, 26)),
                pltpu.SemaphoreType.DMA((max(nx, ny, nz) - 1,)),
                pltpu.SemaphoreType.DMA((nx + ny + nz - 1,)),
            ],
            compiler_params=pltpu.CompilerParams(collective_id=0, has_side_effects=True),
        )(
            rhs[0],
            kappa[0].reshape(16, 32),
            low_ratio.reshape(1, 1),
            high_ratio.reshape(1, 1),
            *[jnp.asarray(c, F32) for c in consts],
            *[jnp.asarray(t) for t in tables],
        )
        return (out[None], est[0, 0])

    return jax.shard_map(
        body,
        mesh=mesh,
        in_specs=(P("wide", "narrow", None, None), P("wide", "narrow", None, None), P(), P()),
        out_specs=(P("wide", "narrow", None, None), P()),
        check_vma=False,
    )
```
